32 devices in a mesh: gx: 4 (over y, x), gy: 8 (over z, core).
Axes of the slice: x: 2, y: 2, z: 4, core: 2. Of those that a mesh axis runs over, the one named last changes fastest.
Arguments:
- density_one: float32 [512, 512, 512], P('gx', 'gy'), may hold values from -6 to 6
- density_two: float32 [512, 512, 512], P('gx', 'gy'), may hold values from -6 to 6
Outputs:
- correlation: float32 [512, 512, 512], P('gx', 'gy')
The draws below stay inside these ranges and needn't reach their ends.
All inputs are finite; a program needn't handle non-finite values.
Results may differ from the reference program's by a relative error of at most 0.00013.
Values sent between devices are 32-bit elements; how exact they have to be, the bound alone decides.
A program may use at most 256 MiB of HBM per device.

```python
import math
import jax
import jax.numpy as jnp

NX = 512
NY = 512
NZ = 512


def levels(stream_key, extent, pieces, low, largest):
    def one(position, parts):
        steps = jax.random.uniform(jax.random.fold_in(jax.random.fold_in(stream_key, 6), position), (parts,), jnp.float32, low / len(pieces), largest / len(pieces))
        return jnp.repeat(jnp.exp(steps), extent[position] // parts).reshape((-1,) + (1,) * (len(extent) - position - 1))

    level = one(*pieces[0])
    for cut in pieces[1:]:
        level = level * one(*cut)
    return level


def normal_values(own_key, extent, scale, reach, cuts=(), kind=jnp.bfloat16):
    result = scale * jax.random.normal(own_key, extent, jnp.float32)
    if cuts:
        result = result * levels(own_key, extent, cuts, -0.22, 0.18)
    return jnp.clip(result, -reach, reach).astype(kind)


def setup_inputs(seed: int = 0) -> dict:
    arg_keys = jax.random.split(jax.random.key(seed), 3)
    return {
        "density_one": normal_values(arg_keys[0], (NX, NY, NZ), 1.0, 6.0, ((0, 4), (1, 8)), jnp.float32),
        "density_two": normal_values(arg_keys[1], (NX, NY, NZ), 1.0, 6.0, ((0, 4), (1, 8)), jnp.float32),
    }


def reference(density_one, density_two):
    cell_total = NX * NY * NZ
    spectrum_one = jnp.fft.rfftn(density_one)
    spectrum_two = jnp.fft.rfftn(density_two)
    power = (spectrum_one.real * spectrum_two.real + spectrum_one.imag * spectrum_two.imag) / cell_total
    wave_x = jnp.arange(NX)[:, None, None]
    wave_y = jnp.arange(NY)[None, :, None]
    wave_z = jnp.arange(NZ // 2 + 1)[None, None, :]
    kept_modes = (wave_x != NX // 2) & (wave_y != NY // 2) & (wave_z != NZ // 2)
    power = jnp.where(kept_modes, power, jnp.zeros_like(power))
    correlation = jnp.fft.irfftn(power * (1.0 + 0j), s=(NX, NY, NZ)) * math.sqrt(cell_total)
    return correlation.astype(jnp.float32)
```

```python
import math

import jax
import jax.numpy as jnp
import numpy as np
from jax import lax
from jax.sharding import PartitionSpec as P

split_mode = lax.Precision.HIGH


def phases(numerator, denominator):
    radians = (numerator % denominator) * (2.0 * math.pi / denominator)
    return np.cos(radians), np.sin(radians)


def base_table(length):
    positions = np.arange(length)
    cosines, sines = phases(positions[:, None] * positions[None, :], length)
    return cosines.astype(np.float32), sines.astype(np.float32)


def complex_table(base, direction):
    cosines, sines = base
    signed = direction * sines
    real_rows = jnp.stack([cosines, signed], axis=1)
    imag_rows = jnp.stack([-signed, cosines], axis=1)
    return jnp.stack([real_rows, imag_rows], axis=0)


def depth_tables(depth_cells, devices, kz_slices, chunk, chunk_slices, scale):
    wave = (
        np.arange(devices)[:, None] * kz_slices
        + chunk * chunk_slices
        + np.arange(chunk_slices)[None, :]
    )
    cosines, sines = phases(wave[:, :, None] * np.arange(depth_cells), depth_cells)
    weight = np.where(wave == 0, 1.0, 2.0)[:, :, None] * scale
    forward = np.stack([cosines, -sines], axis=1).reshape(-1, depth_cells)
    inverse = np.stack([weight * cosines, -weight * sines], axis=1).reshape(-1, depth_cells)
    return forward.astype(np.float32), inverse.astype(np.float32)


def on_device(density_one, density_two):
    count_x = lax.axis_size("gx")
    count_y = lax.axis_size("gy")
    devices = count_x * count_y
    x_local, y_local, depth_cells = density_one.shape
    grid_x = x_local * count_x
    grid_y = y_local * count_y
    kz_slices = depth_cells // 2 // devices
    cell_total = float(grid_x * grid_y * depth_cells)
    chunks = 2 if kz_slices % 2 == 0 else 1
    per_chunk = kz_slices // chunks

    base_x = base_table(grid_x)
    base_y = base_x if grid_y == grid_x else base_table(grid_y)
    x_forward = complex_table(base_x, -1.0).reshape(2, count_x, x_local, 2, grid_x)
    x_inverse = complex_table(base_x, 1.0).reshape(2, grid_x, 2, count_x, x_local)
    y_forward = complex_table(base_y, -1.0).reshape(2, count_y, y_local, 2, grid_y)
    y_inverse = jnp.stack(base_y, axis=1).reshape(grid_y, 2, count_y, y_local)
    tables = [
        depth_tables(depth_cells, devices, kz_slices, chunk, per_chunk, 1.0 / math.sqrt(cell_total))
        for chunk in range(chunks)
    ]
    keep_x = np.arange(grid_x) != grid_x // 2
    keep_y = np.arange(grid_y) != grid_y // 2
    keep = keep_y[:, None, None] & keep_x[None, None, :]

    def exchange(rows):
        return lax.all_to_all(rows, ("gx", "gy"), split_axis=0, concat_axis=0, tiled=True)

    def product(pattern, left, right):
        return jnp.einsum(pattern, left, right, precision=split_mode)

    def depth_forward(density, table):
        lines = product("gz,xyz->gyx", table, density)
        return exchange(lines.reshape(devices, 2 * per_chunk, y_local * x_local))

    def plane_forward(rows):
        rows = rows.reshape(count_x, count_y, 2, per_chunk, y_local, x_local)
        lines = product("dspkyx,pdxrw->skyrw", rows, x_forward)
        return product("skyrw,rsytq->tqkw", lines, y_forward)

    moved = [
        [depth_forward(density, forward) for density in (density_one, density_two)]
        for forward, _ in tables
    ]
    correlation = None
    for (one, two), (_, inverse) in zip(moved, tables):
        first = plane_forward(one)
        second = plane_forward(two)
        power = (first[0] * second[0] + first[1] * second[1]) / cell_total
        power = jnp.where(keep, power, 0.0)
        lines = product("qkw,qrsy->srkyw", power, y_inverse)
        blocks = product("srkyw,rwpdx->dspkyx", lines, x_inverse)
        back = exchange(blocks.reshape(devices, 2 * per_chunk, y_local * x_local))
        back = back.reshape(devices * 2 * per_chunk, y_local, x_local)
        part = product("gyx,gz->xyz", back, inverse)
        correlation = part if correlation is None else correlation + part
    return correlation


def solution(mesh):
    return jax.shard_map(
        on_device,
        mesh=mesh,
        in_specs=(P("gx", "gy", None), P("gx", "gy", None)),
        out_specs=P("gx", "gy", None),
        check_vma=False,
    )
```
